512 devices in a mesh: ab: 16 (over y, x_lo), cd: 32 (over z, x_hi, core).
Axes of the slice: x: 4 (x_hi: 2, x_lo: 2; x = x_hi * 2 + x_lo), y: 8, z: 8, core: 2. Of those that a mesh axis runs over, the one named last changes fastest.
Arguments:
- factors: bfloat16 [128, 128, 2048], P('ab', 'cd'), may hold values from -0.25 to 0.25
- amplitudes: float32 [256, 128, 128], P('cd', 'ab'), may hold values from -4 to 4
- driving: float32 [256, 128, 128], P('cd', 'ab'), may hold values from -8 to 8
- occ_energy: float32 [32], replicated, may hold values from -2 to -0.5
- vir_energy: float32 [128], replicated, may hold values from 0.5 to 3
Outputs:
- new_amplitudes: float32 [256, 128, 128], P('cd', 'ab')
- residual: float32 [256, 128, 128], P('cd', 'ab')
The draws below stay inside these ranges and needn't reach their ends.
All inputs are finite; a program needn't handle non-finite values.
Results may differ from the reference program's by a relative error of at most 0.0036.
Values may be sent and summed in bfloat16 or wider, within the bound.
No kernel may reach another device: no remote copies, remote signals or barrier semaphores. Data moves between devices by JAX's collectives and lax.ppermute only.
A program may use at most 64 MiB of HBM per device.

```python
import jax
import jax.numpy as jnp
from jax import lax

VIRT = 128
AUX = 2048
NOCC = 32
ITERS = 2
OO = 256


def strengthened(array, stream_key, source, target, parts, factor):
    def block_of(position):
        return (jnp.arange(array.shape[position]) // (array.shape[position] // parts)).reshape((-1,) + (1,) * (array.ndim - 1 - position))

    first = jax.random.permutation(stream_key, parts)[block_of(target)]
    other_side = (block_of(target) + parts // 2) % parts
    return jnp.where((block_of(source) == first) | (block_of(source) == other_side), factor * array, array)


def shard_levels(rng, dims, shards, low, largest):
    gain, own = 1.0, jax.random.fold_in(rng, 6)
    for axis_at, parts in shards:
        steps = jnp.exp(jax.random.uniform(jax.random.fold_in(own, axis_at), (parts,), jnp.float32, low / len(shards), largest / len(shards)))
        gain = gain * jnp.repeat(steps, dims[axis_at] // parts).reshape([-1 if axis == axis_at else 1 for axis in range(len(dims))])
    return gain


def scatter_about(rng, shape, deviation, bound, split=(), held_as=jnp.bfloat16):
    result = jax.random.normal(rng, shape, jnp.float32) * deviation
    if len(split) > 0:
        result = shard_levels(rng, shape, split, -0.22, 0.18) * result
    return jnp.clip(result, min=-bound, max=bound).astype(held_as)


def gaussian_with(key, dims, scale, reach, pieces, heavy, held_as=jnp.bfloat16):
    array = scale * jax.random.normal(key, dims, jnp.float32)
    if pieces:
        array = array * shard_levels(key, dims, pieces, -0.22, 0.18)
    return jnp.clip(strengthened(array, jax.random.fold_in(key, 3), *heavy), -reach, reach).astype(held_as)


def setup_inputs(seed: int = 0) -> dict:
    splits = jax.random.split(jax.random.key(seed), 6)
    factors = scatter_about(splits[0], (VIRT, VIRT, AUX), ((2.0 / (VIRT * AUX ** 0.5)) ** 0.5), 0.25, ((0, 16), (1, 32)))
    amplitudes = gaussian_with(splits[1], (OO, VIRT, VIRT), 0.5, 4.0, ((0, 32), (1, 16)), (2, 0, 32, 2.75), jnp.float32)
    driving = scatter_about(splits[2], (OO, VIRT, VIRT), 2.0, 8.0, ((0, 32), (1, 16)), jnp.float32)
    occ_energy = jnp.clip(jax.random.uniform(splits[3], (NOCC,), jnp.float32, -2.0, -0.5), -2.0, -0.5)
    vir_energy = jnp.clip(jax.random.uniform(splits[4], (VIRT,), jnp.float32, 0.5, 3.0), 0.5, 3.0)
    return {"factors": factors, "amplitudes": amplitudes, "driving": driving, "occ_energy": occ_energy, "vir_energy": vir_energy}


def reference(factors, amplitudes, driving, occ_energy, vir_energy):
    n_occ = occ_energy.shape[0]
    pairs = amplitudes.shape[0]
    virtuals = amplitudes.shape[1]
    aux_width = factors.shape[2]
    row_ids = lax.iota(jnp.int32, pairs)
    occ_pair = occ_energy[row_ids // n_occ] + occ_energy[row_ids % n_occ]
    denominator = vir_energy[None, :, None] + vir_energy[None, None, :] - occ_pair[:, None, None]
    right_flat = factors.reshape(virtuals * virtuals, aux_width)
    current = amplitudes
    residual = amplitudes
    for step in range(ITERS):
        rounded = current.astype(jnp.bfloat16).astype(jnp.float32)

        def one_virtual(left):
            tile = lax.dot_general(left, right_flat, (((1,), (1,)), ((), ())), preferred_element_type=jnp.float32)
            tile = tile.astype(jnp.bfloat16).astype(jnp.float32).reshape(virtuals, virtuals, virtuals)
            return jnp.einsum('icd,cbd->ib', rounded, tile)

        stacked = lax.map(one_virtual, factors)
        ladder = jnp.transpose(stacked, (1, 0, 2))
        symmetric = 0.5 * (ladder + jnp.transpose(ladder, (0, 2, 1)))
        residual = driving + denominator * current + symmetric
        current = current - residual / denominator
    return current, residual
```

```python
import jax
import jax.numpy as jnp
from jax import lax
from jax.experimental import pallas as pl
from jax.experimental.pallas import tpu as pltpu
from jax.sharding import Mesh, PartitionSpec as P

ITERS = 2
AB = ("y", "xl")
CD = ("z", "xh", "k")


def pair_layout(stacked, n_cd):
    count, rows, a_local, virtuals = stacked.shape
    width = virtuals // n_cd
    split = stacked.reshape(count, rows, a_local, n_cd, width).transpose(3, 0, 4, 2, 1)
    swapped = lax.all_to_all(split.reshape(n_cd, -1), CD, 0, 0, tiled=True)
    swapped = swapped.reshape(n_cd, count, width * a_local, rows).transpose(1, 2, 0, 3)
    return swapped.reshape(count, width * a_local, n_cd * rows)


def spread(block, n_ab):
    copies = jnp.broadcast_to(block[None], (n_ab,) + block.shape)
    return lax.all_to_all(copies, AB, 0, 0, tiled=True).reshape(-1, block.shape[1])


LANES = 128


def tile_kernel(left_ref, piece_ref, inward_ref, tiles_ref, message_ref, gram_ref, tile_ref, sum_ref):
    n_z, n_k, n_xh, block, aux_width = left_ref.shape
    a_local = 8
    rows = n_z * n_k * n_xh * block
    d_local = piece_ref.shape[0] // LANES
    left = jnp.concatenate(
        [left_ref[z, k, xh] for z in range(n_z) for xh in range(n_xh) for k in range(n_k)], axis=0
    )
    for d in range(d_local):
        gram_ref[d] = lax.dot_general(
            left,
            piece_ref[d * LANES : (d + 1) * LANES, :],
            (((1,), (1,)), ((), ())),
            preferred_element_type=jnp.float32,
        )
    groups = rows // (a_local * 8)
    for a in range(a_local):
        for d in range(d_local):
            part = gram_ref[d, pl.ds(a, rows // a_local, stride=a_local), :]
            tile_ref[:, d, :, a * LANES : (a + 1) * LANES] = part.reshape(groups, 8, LANES)
    tiles = tile_ref[...].reshape(groups * d_local * 8, a_local * LANES).astype(jnp.bfloat16)
    tiles_ref[...] = tiles
    first = pl.program_id(0) == 0
    for half in range(2):
        lanes = inward_ref[:, half * LANES : (half + 1) * LANES]
        for a in range(a_local):
            out = lax.dot_general(
                tiles[:, a * LANES : (a + 1) * LANES],
                lanes,
                (((0,), (0,)), ((), ())),
                preferred_element_type=jnp.float32,
            )
            at = pl.ds(a, LANES, stride=a_local)
            before = sum_ref[half, at, :]
            sum_ref[half, at, :] = jnp.where(first, out, before + out)
        message_ref[:, half * LANES : (half + 1) * LANES] = sum_ref[half].astype(jnp.bfloat16)


def tiles_and_ladder(left, piece, inward):
    n_z, n_k, n_xh, block, aux_width = left.shape
    steps = 2
    contracted = inward.shape[0]
    wide = 8 * LANES
    part = contracted // steps
    d_local = piece.shape[0] // LANES
    return pl.pallas_call(
        tile_kernel,
        grid=(steps,),
        in_specs=[
            pl.BlockSpec((n_z // steps, n_k, n_xh, block, aux_width), lambda s: (s, 0, 0, 0, 0)),
            pl.BlockSpec(piece.shape, lambda s: (0, 0)),
            pl.BlockSpec((part, inward.shape[1]), lambda s: (s, 0)),
        ],
        out_specs=[
            pl.BlockSpec((part, wide), lambda s: (s, 0)),
            pl.BlockSpec((wide, inward.shape[1]), lambda s: (0, 0)),
        ],
        out_shape=[
            jax.ShapeDtypeStruct((contracted, wide), jnp.bfloat16),
            jax.ShapeDtypeStruct((wide, inward.shape[1]), jnp.bfloat16),
        ],
        scratch_shapes=[
            pltpu.VMEM((d_local, 2 * part, LANES), jnp.float32),
            pltpu.VMEM((part // (8 * d_local), d_local, 8, wide), jnp.float32),
            pltpu.VMEM((2, wide, LANES), jnp.float32),
        ],
        name="tiles_and_ladder",
    )(left, piece, inward)


def local(factors, amplitudes, driving, occ_energy, vir_energy):
    rows, a_local, virtuals = amplitudes.shape
    d_local, aux_width = factors.shape[1:]
    n_z, n_xh, n_k = (lax.axis_size(name) for name in CD)
    n_ab, n_cd = virtuals // a_local, virtuals // d_local
    pairs = rows * n_cd
    cd_index = lax.axis_index(CD)
    ab_index = lax.axis_index(AB)

    turned = factors.transpose(1, 0, 2)
    heads = lax.all_gather(turned[None], "xl", axis=0, tiled=True)
    piece = lax.all_gather(heads, "y", axis=0, tiled=True)
    columns = lax.all_gather(turned[None], "xh", axis=0, tiled=True)
    left = lax.all_gather(columns[None], ("z", "k"), axis=0, tiled=True)
    left = left.reshape(n_z, n_k, n_xh, d_local * a_local, aux_width)
    piece = piece.transpose(1, 0, 2, 3).reshape(d_local * virtuals, aux_width)

    n_occ = occ_energy.shape[0]
    occ_pairs = (occ_energy[: pairs // n_occ, None] + occ_energy[None, :]).reshape(pairs)
    occ_rows = lax.dynamic_slice_in_dim(occ_pairs, cd_index * rows, rows)
    vir_a = lax.dynamic_slice_in_dim(vir_energy, ab_index * a_local, a_local)
    vir_d = lax.dynamic_slice_in_dim(vir_energy, cd_index * d_local, d_local)
    denom_rows = vir_a[None, :, None] + vir_energy[None, None, :] - occ_rows[:, None, None]
    vir_block = (vir_d[:, None] + vir_a[None, :]).reshape(-1, 1)
    denom_block = vir_block - occ_pairs[None, :]

    rounded = amplitudes.astype(jnp.bfloat16).astype(jnp.float32)
    both = jnp.stack([amplitudes, driving])
    mirror = lax.all_to_all(both, AB, split_axis=3, concat_axis=2, tiled=True).transpose(0, 1, 3, 2)
    even = 0.5 * (both + mirror)
    even_rounded = 0.5 * (rounded + mirror[0].astype(jnp.bfloat16).astype(jnp.float32))
    blocks = pair_layout(jnp.concatenate([even, even_rounded[None]]), n_cd)
    current, drive = blocks[0], blocks[1]
    inward = spread(blocks[2].astype(jnp.bfloat16), n_ab)

    tiles, first = tiles_and_ladder(left, piece, inward)
    parts = lax.all_to_all(first.reshape(n_cd, -1, pairs), CD, 0, 0, tiled=True)
    ladder = jnp.sum(parts.astype(jnp.float32), axis=0)
    current = current - (drive + denom_block * current + ladder) / denom_block

    inward = spread(current.astype(jnp.bfloat16), n_ab)
    second = lax.dot_general(
        inward, tiles, (((0,), (0,)), ((), ())), preferred_element_type=jnp.float32
    ).astype(jnp.bfloat16)
    high = ladder.astype(jnp.bfloat16)
    low = (ladder - high.astype(jnp.float32)).astype(jnp.bfloat16)
    extra = jnp.stack([high, low]).reshape(2 * ladder.shape[0], n_cd, rows).transpose(1, 2, 0)
    message = jnp.concatenate([second.reshape(n_cd, rows, -1), extra], axis=2)
    parts = lax.all_to_all(message, CD, 0, 0, tiled=True)
    wide = virtuals * a_local
    ladder_second = jnp.sum(parts[:, :, :wide].astype(jnp.float32), axis=0)
    ladder_second = ladder_second.reshape(rows, a_local, virtuals)
    ladder_first = parts[:, :, wide:].astype(jnp.float32).reshape(n_cd, rows, 2, d_local, a_local)
    ladder_first = jnp.sum(ladder_first, axis=2).transpose(1, 3, 0, 2).reshape(rows, a_local, virtuals)

    current = amplitudes - (driving + denom_rows * amplitudes + ladder_first) / denom_rows
    residual = driving + denom_rows * current + ladder_second
    return (current - residual / denom_rows, residual)


def solution(mesh):
    fine = Mesh(mesh.devices.reshape(8, 2, 8, 2, 2), AB + CD)
    placed = (P(AB, CD, None), P(CD, AB, None), P(CD, AB, None), P(), P())
    return jax.shard_map(
        local,
        mesh=fine,
        in_specs=placed,
        out_specs=(P(CD, AB, None), P(CD, AB, None)),
        check_vma=False,
    )
```

```python
import jax
import jax.numpy as jnp
from jax import lax
from jax.experimental import pallas as pl
from jax.experimental.pallas import tpu as pltpu
from jax.sharding import Mesh, PartitionSpec as P

ITERS = 2
AB = ("y", "xl")
CD = ("z", "xh", "k")


def pair_layout(stacked, n_cd):
    count, rows, a_local, virtuals = stacked.shape
    width = virtuals // n_cd
    split = stacked.reshape(count, rows, a_local, n_cd, width).transpose(3, 0, 4, 2, 1)
    swapped = lax.all_to_all(split.reshape(n_cd, -1), CD, 0, 0, tiled=True)
    swapped = swapped.reshape(n_cd, count, width * a_local, rows).transpose(1, 2, 0, 3)
    return swapped.reshape(count, width * a_local, n_cd * rows)


def spread(block, n_ab):
    copies = jnp.broadcast_to(block[None], (n_ab,) + block.shape)
    return lax.all_to_all(copies, AB, 0, 0, tiled=True).reshape(-1, block.shape[1])


LANES = 128


def tile_kernel(left_ref, piece_ref, inward_ref, tiles_ref, message_ref, gram_ref, tile_ref, sum_ref):
    n_z, n_k, n_xh, block, aux_width = left_ref.shape
    a_local = 8
    rows = n_z * n_k * n_xh * block
    d_local = piece_ref.shape[0] // LANES
    left = jnp.concatenate(
        [left_ref[z, k, xh] for z in range(n_z) for xh in range(n_xh) for k in range(n_k)], axis=0
    )
    for d in range(d_local):
        gram_ref[d] = lax.dot_general(
            left,
            piece_ref[d * LANES : (d + 1) * LANES, :],
            (((1,), (1,)), ((), ())),
            preferred_element_type=jnp.float32,
        )
    groups = rows // (a_local * 8)
    for a in range(a_local):
        for d in range(d_local):
            part = gram_ref[d, pl.ds(a, rows // a_local, stride=a_local), :]
            tile_ref[:, d, :, a * LANES : (a + 1) * LANES] = part.reshape(groups, 8, LANES)
    tiles = tile_ref[...].reshape(groups * d_local * 8, a_local * LANES).astype(jnp.bfloat16)
    tiles_ref[...] = tiles
    first = pl.program_id(0) == 0
    for half in range(2):
        lanes = inward_ref[:, half * LANES : (half + 1) * LANES]
        for a in range(a_local):
            out = lax.dot_general(
                tiles[:, a * LANES : (a + 1) * LANES],
                lanes,
                (((0,), (0,)), ((), ())),
                preferred_element_type=jnp.float32,
            )
            at = pl.ds(a, LANES, stride=a_local)
            before = sum_ref[half, at, :]
            sum_ref[half, at, :] = jnp.where(first, out, before + out)
        message_ref[:, half * LANES : (half + 1) * LANES] = sum_ref[half].astype(jnp.bfloat16)


def tiles_and_ladder(left, piece, inward):
    n_z, n_k, n_xh, block, aux_width = left.shape
    steps = 2
    contracted = inward.shape[0]
    wide = 8 * LANES
    part = contracted // steps
    d_local = piece.shape[0] // LANES
    return pl.pallas_call(
        tile_kernel,
        grid=(steps,),
        in_specs=[
            pl.BlockSpec((n_z // steps, n_k, n_xh, block, aux_width), lambda s: (s, 0, 0, 0, 0)),
            pl.BlockSpec(piece.shape, lambda s: (0, 0)),
            pl.BlockSpec((part, inward.shape[1]), lambda s: (s, 0)),
        ],
        out_specs=[
            pl.BlockSpec((part, wide), lambda s: (s, 0)),
            pl.BlockSpec((wide, inward.shape[1]), lambda s: (0, 0)),
        ],
        out_shape=[
            jax.ShapeDtypeStruct((contracted, wide), jnp.bfloat16),
            jax.ShapeDtypeStruct((wide, inward.shape[1]), jnp.bfloat16),
        ],
        scratch_shapes=[
            pltpu.VMEM((d_local, 2 * part, LANES), jnp.float32),
            pltpu.VMEM((part // (8 * d_local), d_local, 8, wide), jnp.float32),
            pltpu.VMEM((2, wide, LANES), jnp.float32),
        ],
        name="tiles_and_ladder",
    )(left, piece, inward)


def local(factors, amplitudes, driving, occ_energy, vir_energy):
    rows, a_local, virtuals = amplitudes.shape
    d_local, aux_width = factors.shape[1:]
    n_z, n_xh, n_k = (lax.axis_size(name) for name in CD)
    n_ab, n_cd = virtuals // a_local, virtuals // d_local
    pairs = rows * n_cd
    cd_index = lax.axis_index(CD)
    ab_index = lax.axis_index(AB)

    turned = factors.transpose(1, 0, 2)
    columns = lax.all_gather(turned[None], "xh", axis=0, tiled=True)
    mine = lax.all_gather(turned[None], "y", axis=0, tiled=True)
    left = lax.all_gather(columns[None], ("z", "k"), axis=0, tiled=True)
    left = left.reshape(n_z, n_k, n_xh, d_local * a_local, aux_width)
    n_occ = occ_energy.shape[0]
    occ_pairs = (occ_energy[: pairs // n_occ, None] + occ_energy[None, :]).reshape(pairs)
    occ_rows = lax.dynamic_slice_in_dim(occ_pairs, cd_index * rows, rows)
    vir_a = lax.dynamic_slice_in_dim(vir_energy, ab_index * a_local, a_local)
    vir_d = lax.dynamic_slice_in_dim(vir_energy, cd_index * d_local, d_local)
    denom_rows = vir_a[None, :, None] + vir_energy[None, None, :] - occ_rows[:, None, None]
    vir_block = (vir_d[:, None] + vir_a[None, :]).reshape(-1, 1)
    denom_block = vir_block - occ_pairs[None, :]

    rounded = amplitudes.astype(jnp.bfloat16).astype(jnp.float32)
    both = jnp.stack([amplitudes, driving])
    mirror = lax.all_to_all(both, AB, split_axis=3, concat_axis=2, tiled=True).transpose(0, 1, 3, 2)
    rounded_mirror = mirror[0].astype(jnp.bfloat16).astype(jnp.float32)
    even = 0.5 * jnp.stack([rounded + rounded_mirror, both[1] + mirror[1]])
    theirs = lax.ppermute(lax.optimization_barrier((mine, even))[0], "xl", [(0, 1), (1, 0)])
    even_member = lax.axis_index("xl") == 0
    piece = jnp.stack(
        [jnp.where(even_member, mine, theirs), jnp.where(even_member, theirs, mine)], axis=1
    )
    piece = piece.transpose(2, 0, 1, 3, 4).reshape(d_local * virtuals, aux_width)
    blocks = pair_layout(even, n_cd)
    current, drive = blocks[0], blocks[1]
    inward = spread(current.astype(jnp.bfloat16), n_ab)

    tiles, first = tiles_and_ladder(left, piece, inward)
    parts = lax.all_to_all(first.reshape(n_cd, -1, pairs), CD, 0, 0, tiled=True)
    ladder = jnp.sum(parts.astype(jnp.float32), axis=0)
    current = current - (drive + denom_block * current + ladder) / denom_block

    inward = spread(current.astype(jnp.bfloat16), n_ab)
    second = lax.dot_general(
        inward, tiles, (((0,), (0,)), ((), ())), preferred_element_type=jnp.float32
    ).astype(jnp.bfloat16)
    high = ladder.astype(jnp.bfloat16)
    low = (ladder - high.astype(jnp.float32)).astype(jnp.bfloat16)
    extra = jnp.stack([high, low]).reshape(2 * ladder.shape[0], n_cd, rows).transpose(1, 2, 0)
    message = jnp.concatenate([second.reshape(n_cd, rows, -1), extra], axis=2)
    parts = lax.all_to_all(message, CD, 0, 0, tiled=True)
    wide = virtuals * a_local
    ladder_second = jnp.sum(parts[:, :, :wide].astype(jnp.float32), axis=0)
    ladder_second = ladder_second.reshape(rows, a_local, virtuals)
    ladder_first = parts[:, :, wide:].astype(jnp.float32).reshape(n_cd, rows, 2, d_local, a_local)
    ladder_first = jnp.sum(ladder_first, axis=2).transpose(1, 3, 0, 2).reshape(rows, a_local, virtuals)

    current = amplitudes - (driving + denom_rows * amplitudes + ladder_first) / denom_rows
    residual = driving + denom_rows * current + ladder_second
    return (current - residual / denom_rows, residual)


def solution(mesh):
    fine = Mesh(mesh.devices.reshape(8, 2, 8, 2, 2), AB + CD)
    placed = (P(AB, CD, None), P(CD, AB, None), P(CD, AB, None), P(), P())
    return jax.shard_map(
        local,
        mesh=fine,
        in_specs=placed,
        out_specs=(P(CD, AB, None), P(CD, AB, None)),
        check_vma=False,
    )
```

```python
import jax
import jax.numpy as jnp
from jax import lax
from jax.experimental import pallas as pl
from jax.experimental.pallas import tpu as pltpu
from jax.sharding import Mesh, PartitionSpec as P


AB = ("y", "xl")
CD = ("z", "xh", "k")


def pair_layout(stacked, n_cd):
    count, rows, a_local, virtuals = stacked.shape
    width = virtuals // n_cd
    split = stacked.reshape(count, rows, a_local, n_cd, width).transpose(3, 0, 4, 2, 1)
    swapped = lax.all_to_all(split.reshape(n_cd, -1), CD, 0, 0, tiled=True)
    swapped = swapped.reshape(n_cd, count, width * a_local, rows).transpose(1, 2, 0, 3)
    return swapped.reshape(count, width * a_local, n_cd * rows)


def spread(block, n_ab):
    copies = jnp.broadcast_to(block[None], (n_ab,) + block.shape)
    return lax.all_to_all(copies, AB, 0, 0, tiled=True).reshape(-1, block.shape[1])


LANES = 128


def tile_kernel(left_ref, piece_ref, inward_ref, tiles_ref, message_ref, gram_ref, tile_ref, sum_ref):
    n_z, n_k, n_xh, block, _ = left_ref.shape
    a_local = 8
    rows = n_z * n_k * n_xh * block
    d_local = piece_ref.shape[0] // LANES
    left = jnp.concatenate(
        [left_ref[z, k, xh] for z in range(n_z) for xh in range(n_xh) for k in range(n_k)], axis=0
    )
    gram = lax.dot_general(
        left, piece_ref[...], (((1,), (1,)), ((), ())), preferred_element_type=jnp.float32
    )
    for d in range(d_local):
        gram_ref[d] = gram[:, d * LANES : (d + 1) * LANES]
    groups = rows // (a_local * 8)
    for a in range(a_local):
        for d in range(d_local):
            part = gram_ref[d, pl.ds(a, rows // a_local, stride=a_local), :]
            tile_ref[:, d, :, a * LANES : (a + 1) * LANES] = part.reshape(groups, 8, LANES)
    tiles = tile_ref[...].reshape(groups * d_local * 8, a_local * LANES).astype(jnp.bfloat16)
    tiles_ref[...] = tiles
    first = pl.program_id(0) == 0
    product = lax.dot_general(
        tiles, inward_ref[...], (((0,), (0,)), ((), ())), preferred_element_type=jnp.float32
    )
    for half in range(2):
        lanes = slice(half * LANES, (half + 1) * LANES)
        for a in range(a_local):
            out = product[a * LANES : (a + 1) * LANES, lanes]
            at = pl.ds(a, LANES, stride=a_local)
            before = sum_ref[half, at, :]
            sum_ref[half, at, :] = jnp.where(first, out, before + out)
        message_ref[:, lanes] = sum_ref[half].astype(jnp.bfloat16)


def tiles_and_ladder(left, piece, inward):
    n_z, n_k, n_xh, block, aux_width = left.shape
    steps = 2
    contracted = inward.shape[0]
    wide = 8 * LANES
    part = contracted // steps
    d_local = piece.shape[0] // LANES
    return pl.pallas_call(
        tile_kernel,
        grid=(steps,),
        in_specs=[
            pl.BlockSpec((n_z // steps, n_k, n_xh, block, aux_width), lambda s: (s, 0, 0, 0, 0)),
            pl.BlockSpec(memory_space=pltpu.VMEM),
            pl.BlockSpec((part, inward.shape[1]), lambda s: (s, 0)),
        ],
        out_specs=[
            pl.BlockSpec((part, wide), lambda s: (s, 0)),
            pl.BlockSpec((wide, inward.shape[1]), lambda s: (0, 0)),
        ],
        out_shape=[
            jax.ShapeDtypeStruct((contracted, wide), jnp.bfloat16),
            jax.ShapeDtypeStruct((wide, inward.shape[1]), jnp.bfloat16),
        ],
        scratch_shapes=[
            pltpu.VMEM((d_local, 2 * part, LANES), jnp.float32),
            pltpu.VMEM((part // (8 * d_local), d_local, 8, wide), jnp.float32),
            pltpu.VMEM((2, wide, LANES), jnp.float32),
        ],
        name="tiles_and_ladder",
    )(left, piece, inward)


def local(factors, amplitudes, driving, occ_energy, vir_energy):
    rows, a_local, virtuals = amplitudes.shape
    d_local, aux_width = factors.shape[1:]
    n_z, n_xh, n_k = (lax.axis_size(name) for name in CD)
    n_ab, n_cd = virtuals // a_local, virtuals // d_local
    pairs = rows * n_cd
    cd_index = lax.axis_index(CD)
    ab_index = lax.axis_index(AB)

    turned = factors.transpose(1, 0, 2)
    columns = lax.all_gather(turned[None], "xh", axis=0, tiled=True)
    mine = lax.all_gather(turned[None], "y", axis=0, tiled=True)
    left = lax.all_gather(columns[None], ("z", "k"), axis=0, tiled=True)
    left = left.reshape(n_z, n_k, n_xh, d_local * a_local, aux_width)
    n_occ = occ_energy.shape[0]
    occ_pairs = (occ_energy[: pairs // n_occ, None] + occ_energy[None, :]).reshape(pairs)
    occ_rows = lax.dynamic_slice_in_dim(occ_pairs, cd_index * rows, rows)
    vir_a = lax.dynamic_slice_in_dim(vir_energy, ab_index * a_local, a_local)
    vir_d = lax.dynamic_slice_in_dim(vir_energy, cd_index * d_local, d_local)
    denom_rows = vir_a[None, :, None] + vir_energy[None, None, :] - occ_rows[:, None, None]
    vir_block = (vir_d[:, None] + vir_a[None, :]).reshape(-1, 1)
    denom_block = vir_block - occ_pairs[None, :]

    rounded = amplitudes.astype(jnp.bfloat16).astype(jnp.float32)
    both = jnp.stack([amplitudes, driving])
    mirror = lax.all_to_all(both, AB, split_axis=3, concat_axis=2, tiled=True).transpose(0, 1, 3, 2)
    rounded_mirror = mirror[0].astype(jnp.bfloat16).astype(jnp.float32)
    even = 0.5 * jnp.stack([rounded + rounded_mirror, both[1] + mirror[1]])
    theirs = lax.ppermute(mine, "xl", [(0, 1), (1, 0)])
    even_member = lax.axis_index("xl") == 0
    piece = jnp.stack(
        [jnp.where(even_member, mine, theirs), jnp.where(even_member, theirs, mine)], axis=1
    )
    piece = piece.transpose(2, 0, 1, 3, 4).reshape(d_local * virtuals, aux_width)
    blocks = pair_layout(even, n_cd)
    current, drive = blocks[0], blocks[1]
    inward = spread(current.astype(jnp.bfloat16), n_ab)

    tiles, first = tiles_and_ladder(left, piece, inward)
    parts = lax.all_to_all(first.reshape(n_cd, -1, pairs), CD, 0, 0, tiled=True)
    ladder = jnp.sum(parts.astype(jnp.float32), axis=0)
    current = current - (drive + denom_block * current + ladder) / denom_block

    inward = spread(current.astype(jnp.bfloat16), n_ab)
    second = lax.dot_general(
        inward, tiles, (((0,), (0,)), ((), ())), preferred_element_type=jnp.float32
    ).astype(jnp.bfloat16)
    high = ladder.astype(jnp.bfloat16)
    low = (ladder - high.astype(jnp.float32)).astype(jnp.bfloat16)
    extra = jnp.stack([high, low]).reshape(2 * ladder.shape[0], n_cd, rows).transpose(1, 2, 0)
    message = jnp.concatenate([second.reshape(n_cd, rows, -1), extra], axis=2)
    parts = lax.all_to_all(message, CD, 0, 0, tiled=True)
    wide = virtuals * a_local
    ladder_second = jnp.sum(parts[:, :, :wide].astype(jnp.float32), axis=0)
    ladder_second = ladder_second.reshape(rows, a_local, virtuals)
    ladder_first = parts[:, :, wide:].astype(jnp.float32).reshape(n_cd, rows, 2, d_local, a_local)
    ladder_first = jnp.sum(ladder_first, axis=2).transpose(1, 3, 0, 2).reshape(rows, a_local, virtuals)

    current = amplitudes - (driving + denom_rows * amplitudes + ladder_first) / denom_rows
    residual = driving + denom_rows * current + ladder_second
    return (current - residual / denom_rows, residual)


def solution(mesh):
    fine = Mesh(mesh.devices.reshape(8, 2, 8, 2, 2), AB + CD)
    placed = (P(AB, CD, None), P(CD, AB, None), P(CD, AB, None), P(), P())
    return jax.shard_map(
        local,
        mesh=fine,
        in_specs=placed,
        out_specs=(P(CD, AB, None), P(CD, AB, None)),
        check_vma=False,
    )
```

```python
import jax
import jax.numpy as jnp
from jax import lax
from jax.experimental import pallas as pl
from jax.experimental.pallas import tpu as pltpu
from jax.sharding import Mesh, PartitionSpec as P


AB = ("y", "xl")
CD = ("z", "xh", "k")


def pair_layout(stacked, n_cd):
    count, rows, a_local, virtuals = stacked.shape
    width = virtuals // n_cd
    split = stacked.reshape(count, rows, a_local, n_cd, width).transpose(3, 0, 4, 2, 1)
    swapped = lax.all_to_all(split.reshape(n_cd, -1), CD, 0, 0, tiled=True)
    swapped = swapped.reshape(n_cd, count, width * a_local, rows).transpose(1, 2, 0, 3)
    return swapped.reshape(count, width * a_local, n_cd * rows)


def spread(block, n_ab):
    copies = jnp.broadcast_to(block[None], (n_ab,) + block.shape)
    return lax.all_to_all(copies, AB, 0, 0, tiled=True).reshape(-1, block.shape[1])


LANES = 128
SHIFTS = (0, 4, 3, -3, 2, -2, 1, -1)


def tile_kernel(y_ref, left_ref, inward_ref, *refs):
    n_blocks = len(SHIFTS)
    block_refs, (tiles_ref, message_ref, piece_ref, gram_ref, tile_ref, sum_ref) = refs[:n_blocks], refs[n_blocks:]
    n_z, n_k, n_xh, block, aux_width = left_ref.shape
    a_local = 8
    rows = n_z * n_k * n_xh * block
    n_xl, d_local, b_local, _ = block_refs[0].shape

    @pl.when(pl.program_id(0) == 0)
    def _():
        for shift, block_ref in zip(SHIFTS, block_refs):
            y = (y_ref[0] + n_blocks - shift) % n_blocks
            for d in range(d_local):
                for xl in range(n_xl):
                    piece_ref[d, y, xl * b_local : (xl + 1) * b_local, :] = block_ref[xl, d]

    left = jnp.concatenate(
        [left_ref[z, k, xh] for z in range(n_z) for xh in range(n_xh) for k in range(n_k)], axis=0
    )
    gram = lax.dot_general(
        left, piece_ref[...].reshape(d_local * LANES, aux_width), (((1,), (1,)), ((), ())), preferred_element_type=jnp.float32
    )
    for d in range(d_local):
        gram_ref[d] = gram[:, d * LANES : (d + 1) * LANES]
    groups = rows // (a_local * 8)
    for a in range(a_local):
        for d in range(d_local):
            part = gram_ref[d, pl.ds(a, rows // a_local, stride=a_local), :]
            tile_ref[:, d, :, a * LANES : (a + 1) * LANES] = part.reshape(groups, 8, LANES)
    tiles = tile_ref[...].reshape(groups * d_local * 8, a_local * LANES).astype(jnp.bfloat16)
    tiles_ref[...] = tiles
    first = pl.program_id(0) == 0
    product = lax.dot_general(
        tiles, inward_ref[...], (((0,), (0,)), ((), ())), preferred_element_type=jnp.float32
    )
    for half in range(2):
        lanes = slice(half * LANES, (half + 1) * LANES)
        for a in range(a_local):
            out = product[a * LANES : (a + 1) * LANES, lanes]
            at = pl.ds(a, LANES, stride=a_local)
            before = sum_ref[half, at, :]
            sum_ref[half, at, :] = jnp.where(first, out, before + out)
        message_ref[:, lanes] = sum_ref[half].astype(jnp.bfloat16)


def tiles_and_ladder(y_index, left, inward, blocks):
    n_z, n_k, n_xh, block, aux_width = left.shape
    steps = 2
    contracted = inward.shape[0]
    wide = 8 * LANES
    part = contracted // steps
    n_xl, d_local, b_local, _ = blocks[0].shape
    return pl.pallas_call(
        tile_kernel,
        grid=(steps,),
        in_specs=[
            pl.BlockSpec(memory_space=pltpu.SMEM),
            pl.BlockSpec((n_z // steps, n_k, n_xh, block, aux_width), lambda s: (s, 0, 0, 0, 0)),
            pl.BlockSpec((part, inward.shape[1]), lambda s: (s, 0)),
        ]
        + [pl.BlockSpec(blocks[0].shape, lambda s: (0, 0, 0, 0), pipeline_mode=pl.Buffered(1)) for _ in blocks],
        out_specs=[
            pl.BlockSpec((part, wide), lambda s: (s, 0)),
            pl.BlockSpec((wide, inward.shape[1]), lambda s: (0, 0)),
        ],
        out_shape=[
            jax.ShapeDtypeStruct((contracted, wide), jnp.bfloat16),
            jax.ShapeDtypeStruct((wide, inward.shape[1]), jnp.bfloat16),
        ],
        scratch_shapes=[
            pltpu.VMEM((d_local, len(blocks), n_xl * b_local, aux_width), jnp.bfloat16),
            pltpu.VMEM((d_local, 2 * part, LANES), jnp.float32),
            pltpu.VMEM((part // (8 * d_local), d_local, 8, wide), jnp.float32),
            pltpu.VMEM((2, wide, LANES), jnp.float32),
        ],
        name="tiles_and_ladder",
    )(y_index.reshape(1), left, inward, *blocks)


def local(factors, amplitudes, driving, occ_energy, vir_energy):
    rows, a_local, virtuals = amplitudes.shape
    d_local, aux_width = factors.shape[1:]
    n_z, n_xh, n_k = (lax.axis_size(name) for name in CD)
    n_ab, n_cd = virtuals // a_local, virtuals // d_local
    pairs = rows * n_cd
    cd_index = lax.axis_index(CD)
    ab_index = lax.axis_index(AB)

    turned = factors.transpose(1, 0, 2)
    theirs = lax.ppermute(turned, "xl", [(0, 1), (1, 0)])
    columns = lax.all_gather(turned[None], "xh", axis=0, tiled=True)
    left = lax.all_gather(columns[None], ("z", "k"), axis=0, tiled=True)
    left = left.reshape(n_z, n_k, n_xh, d_local * a_local, aux_width)
    even_member = lax.axis_index("xl") == 0
    pair = jnp.stack([jnp.where(even_member, turned, theirs), jnp.where(even_member, theirs, turned)])
    n_y = lax.axis_size("y")
    y_blocks = [pair]
    for shift in SHIFTS[1:]:
        y_blocks.append(lax.ppermute(pair, "y", [(i, (i + shift) % n_y) for i in range(n_y)]))

    n_occ = occ_energy.shape[0]
    occ_pairs = (occ_energy[: pairs // n_occ, None] + occ_energy[None, :]).reshape(pairs)
    occ_rows = lax.dynamic_slice_in_dim(occ_pairs, cd_index * rows, rows)
    vir_a = lax.dynamic_slice_in_dim(vir_energy, ab_index * a_local, a_local)
    vir_d = lax.dynamic_slice_in_dim(vir_energy, cd_index * d_local, d_local)
    denom_rows = vir_a[None, :, None] + vir_energy[None, None, :] - occ_rows[:, None, None]
    vir_block = (vir_d[:, None] + vir_a[None, :]).reshape(-1, 1)
    denom_block = vir_block - occ_pairs[None, :]

    rounded = amplitudes.astype(jnp.bfloat16).astype(jnp.float32)
    both = jnp.stack([amplitudes, driving])
    mirror = lax.all_to_all(both, AB, split_axis=3, concat_axis=2, tiled=True)
    mirror = mirror.transpose(0, 1, 3, 2)
    rounded_mirror = mirror[0].astype(jnp.bfloat16).astype(jnp.float32)
    even = 0.5 * jnp.stack([rounded + rounded_mirror, both[1] + mirror[1]])
    blocks = pair_layout(even, n_cd)
    current, drive = blocks[0], blocks[1]
    inward = spread(current.astype(jnp.bfloat16), n_ab)

    tiles, first = tiles_and_ladder(lax.axis_index("y"), left, inward, y_blocks)
    parts = lax.all_to_all(first.reshape(n_cd, -1, pairs), CD, 0, 0, tiled=True)
    ladder = jnp.sum(parts.astype(jnp.float32), axis=0)
    current = current - (drive + denom_block * current + ladder) / denom_block

    inward = spread(current.astype(jnp.bfloat16), n_ab)
    second = lax.dot_general(
        inward, tiles, (((0,), (0,)), ((), ())), preferred_element_type=jnp.float32
    ).astype(jnp.bfloat16)
    high = ladder.astype(jnp.bfloat16)
    low = (ladder - high.astype(jnp.float32)).astype(jnp.bfloat16)
    extra = jnp.stack([high, low]).reshape(2 * ladder.shape[0], n_cd, rows).transpose(1, 2, 0)
    message = jnp.concatenate([second.reshape(n_cd, rows, -1), extra], axis=2)
    parts = lax.all_to_all(message, CD, 0, 0, tiled=True)
    wide = virtuals * a_local
    ladder_second = jnp.sum(parts[:, :, :wide].astype(jnp.float32), axis=0)
    ladder_second = ladder_second.reshape(rows, a_local, virtuals)
    ladder_first = parts[:, :, wide:].astype(jnp.float32).reshape(n_cd, rows, 2, d_local, a_local)
    ladder_first = jnp.sum(ladder_first, axis=2).transpose(1, 3, 0, 2).reshape(rows, a_local, virtuals)

    current = amplitudes - (driving + denom_rows * amplitudes + ladder_first) / denom_rows
    residual = driving + denom_rows * current + ladder_second
    return (current - residual / denom_rows, residual)


def solution(mesh):
    fine = Mesh(mesh.devices.reshape(8, 2, 8, 2, 2), AB + CD)
    placed = (P(AB, CD, None), P(CD, AB, None), P(CD, AB, None), P(), P())
    return jax.shard_map(
        local,
        mesh=fine,
        in_specs=placed,
        out_specs=(P(CD, AB, None), P(CD, AB, None)),
        check_vma=False,
    )
```

```python
import jax
import jax.numpy as jnp
from jax import lax
from jax.experimental import pallas as pl
from jax.experimental.pallas import tpu as pltpu
from jax.sharding import Mesh, PartitionSpec as P


AB = ("y", "xl")
CD = ("z", "xh", "k")


def pair_layout(stacked, n_cd):
    count, rows, a_local, virtuals = stacked.shape
    width = virtuals // n_cd
    split = stacked.reshape(count, rows, a_local, n_cd, width).transpose(3, 0, 4, 2, 1)
    swapped = lax.all_to_all(split.reshape(n_cd, -1), CD, 0, 0, tiled=True)
    swapped = swapped.reshape(n_cd, count, width * a_local, rows).transpose(1, 2, 0, 3)
    return swapped.reshape(count, width * a_local, n_cd * rows)


def spread(block, n_ab):
    copies = jnp.broadcast_to(block[None], (n_ab,) + block.shape)
    return lax.all_to_all(copies, AB, 0, 0, tiled=True).reshape(-1, block.shape[1])


LANES = 128
SHIFTS = ((0,), (4,), (2,), (-2,), (1, 5), (-1, 3))


def tile_kernel(y_ref, left_ref, inward_ref, *refs):
    n_blocks = len(SHIFTS)
    block_refs, (tiles_ref, message_ref, piece_ref, gram_ref, tile_ref, sum_ref) = refs[:n_blocks], refs[n_blocks:]
    n_z, n_k, n_xh, block, aux_width = left_ref.shape
    a_local = 8
    rows = n_z * n_k * n_xh * block
    _, n_xl, d_local, b_local, _ = block_refs[0].shape
    n_y = piece_ref.shape[1]

    @pl.when(pl.program_id(0) == 0)
    def _():
        for shifts, block_ref in zip(SHIFTS, block_refs):
            for slot, shift in enumerate(shifts):
                y = (y_ref[0] + n_y - shift) % n_y
                for d in range(d_local):
                    for xl in range(n_xl):
                        rows_at = slice(xl * b_local, (xl + 1) * b_local)
                        piece_ref[d, y, rows_at, :] = block_ref[slot, xl, d]

    left = jnp.concatenate(
        [left_ref[z, k, xh] for z in range(n_z) for xh in range(n_xh) for k in range(n_k)], axis=0
    )
    gram = lax.dot_general(
        left, piece_ref[...].reshape(d_local * LANES, aux_width), (((1,), (1,)), ((), ())), preferred_element_type=jnp.float32
    )
    for d in range(d_local):
        gram_ref[d] = gram[:, d * LANES : (d + 1) * LANES]
    groups = rows // (a_local * 8)
    for a in range(a_local):
        for d in range(d_local):
            part = gram_ref[d, pl.ds(a, rows // a_local, stride=a_local), :]
            tile_ref[:, d, :, a * LANES : (a + 1) * LANES] = part.reshape(groups, 8, LANES)
    tiles = tile_ref[...].reshape(groups * d_local * 8, a_local * LANES).astype(jnp.bfloat16)
    tiles_ref[...] = tiles
    first = pl.program_id(0) == 0
    product = lax.dot_general(
        tiles, inward_ref[...], (((0,), (0,)), ((), ())), preferred_element_type=jnp.float32
    )
    for half in range(2):
        lanes = slice(half * LANES, (half + 1) * LANES)
        for a in range(a_local):
            out = product[a * LANES : (a + 1) * LANES, lanes]
            at = pl.ds(a, LANES, stride=a_local)
            before = sum_ref[half, at, :]
            sum_ref[half, at, :] = jnp.where(first, out, before + out)
        message_ref[:, lanes] = sum_ref[half].astype(jnp.bfloat16)


def tiles_and_ladder(y_index, left, inward, blocks):
    n_z, n_k, n_xh, block, aux_width = left.shape
    steps = 2
    contracted = inward.shape[0]
    wide = 8 * LANES
    part = contracted // steps
    _, n_xl, d_local, b_local, _ = blocks[0].shape
    n_y = sum(block.shape[0] for block in blocks)
    return pl.pallas_call(
        tile_kernel,
        grid=(steps,),
        in_specs=[
            pl.BlockSpec(memory_space=pltpu.SMEM),
            pl.BlockSpec((n_z // steps, n_k, n_xh, block, aux_width), lambda s: (s, 0, 0, 0, 0)),
            pl.BlockSpec((part, inward.shape[1]), lambda s: (s, 0)),
        ]
        + [pl.BlockSpec(block.shape, lambda s: (0,) * 5, pipeline_mode=pl.Buffered(1)) for block in blocks],
        out_specs=[
            pl.BlockSpec((part, wide), lambda s: (s, 0)),
            pl.BlockSpec((wide, inward.shape[1]), lambda s: (0, 0)),
        ],
        out_shape=[
            jax.ShapeDtypeStruct((contracted, wide), jnp.bfloat16),
            jax.ShapeDtypeStruct((wide, inward.shape[1]), jnp.bfloat16),
        ],
        scratch_shapes=[
            pltpu.VMEM((d_local, n_y, n_xl * b_local, aux_width), jnp.bfloat16),
            pltpu.VMEM((d_local, 2 * part, LANES), jnp.float32),
            pltpu.VMEM((part // (8 * d_local), d_local, 8, wide), jnp.float32),
            pltpu.VMEM((2, wide, LANES), jnp.float32),
        ],
        name="tiles_and_ladder",
    )(y_index.reshape(1), left, inward, *blocks)


def local(factors, amplitudes, driving, occ_energy, vir_energy):
    rows, a_local, virtuals = amplitudes.shape
    d_local, aux_width = factors.shape[1:]
    n_z, n_xh, n_k = (lax.axis_size(name) for name in CD)
    n_ab, n_cd = virtuals // a_local, virtuals // d_local
    pairs = rows * n_cd
    cd_index = lax.axis_index(CD)
    ab_index = lax.axis_index(AB)

    turned = factors.transpose(1, 0, 2)
    theirs = lax.ppermute(turned, "xl", [(0, 1), (1, 0)])
    columns = lax.all_gather(turned[None], "xh", axis=0, tiled=True)
    left = lax.all_gather(columns[None], ("z", "k"), axis=0, tiled=True)
    left = left.reshape(n_z, n_k, n_xh, d_local * a_local, aux_width)
    even_member = lax.axis_index("xl") == 0
    pair = jnp.stack([jnp.where(even_member, turned, theirs), jnp.where(even_member, theirs, turned)])
    n_y = lax.axis_size("y")

    def shifted(value, shift):
        return lax.ppermute(value, "y", [(i, (i + shift) % n_y) for i in range(n_y)])

    pair = pair[None]
    opposite = shifted(pair, 4)
    two = jnp.concatenate([pair, opposite])
    y_blocks = [pair, opposite, shifted(pair, 2), shifted(pair, -2), shifted(two, 1), shifted(two, -1)]

    n_occ = occ_energy.shape[0]
    occ_pairs = (occ_energy[: pairs // n_occ, None] + occ_energy[None, :]).reshape(pairs)
    occ_rows = lax.dynamic_slice_in_dim(occ_pairs, cd_index * rows, rows)
    vir_a = lax.dynamic_slice_in_dim(vir_energy, ab_index * a_local, a_local)
    vir_d = lax.dynamic_slice_in_dim(vir_energy, cd_index * d_local, d_local)
    denom_rows = vir_a[None, :, None] + vir_energy[None, None, :] - occ_rows[:, None, None]
    vir_block = (vir_d[:, None] + vir_a[None, :]).reshape(-1, 1)
    denom_block = vir_block - occ_pairs[None, :]

    rounded = amplitudes.astype(jnp.bfloat16).astype(jnp.float32)
    both = jnp.stack([amplitudes, driving])
    mirror = lax.all_to_all(both, AB, split_axis=3, concat_axis=2, tiled=True)
    mirror = mirror.transpose(0, 1, 3, 2)
    rounded_mirror = mirror[0].astype(jnp.bfloat16).astype(jnp.float32)
    even = 0.5 * jnp.stack([rounded + rounded_mirror, both[1] + mirror[1]])
    blocks = pair_layout(even, n_cd)
    current, drive = blocks[0], blocks[1]
    inward = spread(current.astype(jnp.bfloat16), n_ab)

    tiles, first = tiles_and_ladder(lax.axis_index("y"), left, inward, y_blocks)
    parts = lax.all_to_all(first.reshape(n_cd, -1, pairs), CD, 0, 0, tiled=True)
    ladder = jnp.sum(parts.astype(jnp.float32), axis=0)
    current = current - (drive + denom_block * current + ladder) / denom_block

    inward = spread(current.astype(jnp.bfloat16), n_ab)
    second = lax.dot_general(
        inward, tiles, (((0,), (0,)), ((), ())), preferred_element_type=jnp.float32
    ).astype(jnp.bfloat16)
    high = ladder.astype(jnp.bfloat16)
    low = (ladder - high.astype(jnp.float32)).astype(jnp.bfloat16)
    extra = jnp.stack([high, low]).reshape(2 * ladder.shape[0], n_cd, rows).transpose(1, 2, 0)
    message = jnp.concatenate([second.reshape(n_cd, rows, -1), extra], axis=2)
    parts = lax.all_to_all(message, CD, 0, 0, tiled=True)
    wide = virtuals * a_local
    ladder_second = jnp.sum(parts[:, :, :wide].astype(jnp.float32), axis=0)
    ladder_second = ladder_second.reshape(rows, a_local, virtuals)
    ladder_first = parts[:, :, wide:].astype(jnp.float32).reshape(n_cd, rows, 2, d_local, a_local)
    ladder_first = jnp.sum(ladder_first, axis=2).transpose(1, 3, 0, 2).reshape(rows, a_local, virtuals)

    current = amplitudes - (driving + denom_rows * amplitudes + ladder_first) / denom_rows
    residual = driving + denom_rows * current + ladder_second
    return (current - residual / denom_rows, residual)


def solution(mesh):
    fine = Mesh(mesh.devices.reshape(8, 2, 8, 2, 2), AB + CD)
    placed = (P(AB, CD, None), P(CD, AB, None), P(CD, AB, None), P(), P())
    return jax.shard_map(
        local,
        mesh=fine,
        in_specs=placed,
        out_specs=(P(CD, AB, None), P(CD, AB, None)),
        check_vma=False,
    )
```

```python
import jax
import jax.numpy as jnp
from jax import lax
from jax.experimental import pallas as pl
from jax.experimental.pallas import tpu as pltpu
from jax.sharding import Mesh, PartitionSpec as P


AB = ("y", "xl")
CD = ("z", "xh", "k")


def pair_layout(stacked, n_cd):
    count, rows, a_local, virtuals = stacked.shape
    width = virtuals // n_cd
    split = stacked.reshape(count, rows, a_local, n_cd, width).transpose(3, 0, 4, 2, 1)
    swapped = lax.all_to_all(split.reshape(n_cd, -1), CD, 0, 0, tiled=True)
    swapped = swapped.reshape(n_cd, count, width * a_local, rows).transpose(1, 2, 0, 3)
    return swapped.reshape(count, width * a_local, n_cd * rows)


def spread(block, n_ab):
    copies = jnp.broadcast_to(block[None], (n_ab,) + block.shape)
    return lax.all_to_all(copies, AB, 0, 0, tiled=True).reshape(-1, block.shape[1])


LANES = 128
SHIFTS = ((0,), (4,), (2,), (-2,), (1, 5), (-1, 3))


def tile_kernel(at_ref, left_ref, inward_ref, *refs):
    n_blocks = len(SHIFTS)
    block_refs, (tiles_ref, kept_ref, sent_ref, piece_ref, gram_ref, tile_ref, sum_ref) = refs[:n_blocks], refs[n_blocks:]
    n_z, n_k, n_xh, block, aux_width = left_ref.shape
    a_local = 8
    rows = n_z * n_k * n_xh * block
    _, n_xl, d_local, b_local, _ = block_refs[0].shape
    n_y = piece_ref.shape[1]

    @pl.when(pl.program_id(0) == 0)
    def _():
        for shifts, block_ref in zip(SHIFTS, block_refs):
            for slot, shift in enumerate(shifts):
                y = (at_ref[0] + n_y - shift) % n_y
                for d in range(d_local):
                    for xl in range(n_xl):
                        rows_at = slice(xl * b_local, (xl + 1) * b_local)
                        piece_ref[d, y, rows_at, :] = block_ref[slot, xl, d]

    left = jnp.concatenate(
        [left_ref[z, k, xh] for z in range(n_z) for xh in range(n_xh) for k in range(n_k)], axis=0
    )
    gram = lax.dot_general(
        left, piece_ref[...].reshape(d_local * LANES, aux_width), (((1,), (1,)), ((), ())), preferred_element_type=jnp.float32
    )
    for d in range(d_local):
        gram_ref[d] = gram[:, d * LANES : (d + 1) * LANES]
    groups = rows // (a_local * 8)
    for a in range(a_local):
        for d in range(d_local):
            part = gram_ref[d, pl.ds(a, rows // a_local, stride=a_local), :]
            tile_ref[:, d, :, a * LANES : (a + 1) * LANES] = part.reshape(groups, 8, LANES)
    tiles = tile_ref[...].reshape(groups * d_local * 8, a_local * LANES).astype(jnp.bfloat16)
    tiles_ref[...] = tiles
    first = pl.program_id(0) == 0
    product = lax.dot_general(
        tiles, inward_ref[...], (((0,), (0,)), ((), ())), preferred_element_type=jnp.float32
    )
    for half in range(2):
        lanes = slice(half * LANES, (half + 1) * LANES)
        for a in range(a_local):
            out = product[a * LANES : (a + 1) * LANES, lanes]
            at = pl.ds(a, LANES, stride=a_local)
            before = sum_ref[half, at, :]
            sum_ref[half, at, :] = jnp.where(first, out, before + out)
        n_groups, size, _ = kept_ref.shape
        for group in range(n_groups):
            own = pl.multiple_of((2 * group + at_ref[1]) * size, size)
            other = pl.multiple_of((2 * group + 1 - at_ref[1]) * size, size)
            kept_ref[group, :, lanes] = sum_ref[half, pl.ds(own, size), :]
            sent_ref[group, :, lanes] = sum_ref[half, pl.ds(other, size), :].astype(jnp.bfloat16)


def tiles_and_ladder(place, left, inward, blocks):
    n_z, n_k, n_xh, block, aux_width = left.shape
    steps = 2
    contracted = inward.shape[0]
    wide = 8 * LANES
    part = contracted // steps
    halves = (n_z * n_xh, wide // (n_z * n_xh * n_k), inward.shape[1])
    _, n_xl, d_local, b_local, _ = blocks[0].shape
    n_y = sum(block.shape[0] for block in blocks)
    return pl.pallas_call(
        tile_kernel,
        grid=(steps,),
        in_specs=[
            pl.BlockSpec(memory_space=pltpu.SMEM),
            pl.BlockSpec((n_z // steps, n_k, n_xh, block, aux_width), lambda s: (s, 0, 0, 0, 0)),
            pl.BlockSpec((part, inward.shape[1]), lambda s: (s, 0)),
        ]
        + [pl.BlockSpec(block.shape, lambda s: (0,) * 5, pipeline_mode=pl.Buffered(1)) for block in blocks],
        out_specs=[
            pl.BlockSpec((part, wide), lambda s: (s, 0)),
            pl.BlockSpec(halves, lambda s: (0, 0, 0)),
            pl.BlockSpec(halves, lambda s: (0, 0, 0)),
        ],
        out_shape=[
            jax.ShapeDtypeStruct((contracted, wide), jnp.bfloat16),
            jax.ShapeDtypeStruct(halves, jnp.float32),
            jax.ShapeDtypeStruct(halves, jnp.bfloat16),
        ],
        scratch_shapes=[
            pltpu.VMEM((d_local, n_y, n_xl * b_local, aux_width), jnp.bfloat16),
            pltpu.VMEM((d_local, 2 * part, LANES), jnp.float32),
            pltpu.VMEM((part // (8 * d_local), d_local, 8, wide), jnp.float32),
            pltpu.VMEM((2, wide, LANES), jnp.float32),
        ],
        name="tiles_and_ladder",
    )(place, left, inward, *blocks)


def local(factors, amplitudes, driving, occ_energy, vir_energy):
    rows, a_local, virtuals = amplitudes.shape
    d_local, aux_width = factors.shape[1:]
    n_z, n_xh, n_k = (lax.axis_size(name) for name in CD)
    n_ab, n_cd = virtuals // a_local, virtuals // d_local
    pairs = rows * n_cd
    cd_index = lax.axis_index(CD)
    ab_index = lax.axis_index(AB)

    turned = factors.transpose(1, 0, 2)
    theirs = lax.ppermute(turned, "xl", [(0, 1), (1, 0)])
    columns = lax.all_gather(turned[None], "xh", axis=0, tiled=True)
    left = lax.all_gather(columns[None], ("z", "k"), axis=0, tiled=True)
    left = left.reshape(n_z, n_k, n_xh, d_local * a_local, aux_width)
    even_member = lax.axis_index("xl") == 0
    pair = jnp.stack([jnp.where(even_member, turned, theirs), jnp.where(even_member, theirs, turned)])
    n_y = lax.axis_size("y")

    def shifted(value, shift):
        return lax.ppermute(value, "y", [(i, (i + shift) % n_y) for i in range(n_y)])

    pair = pair[None]
    opposite = shifted(pair, 4)
    two = jnp.concatenate([pair, opposite])
    y_blocks = [pair, opposite, shifted(pair, 2), shifted(pair, -2), shifted(two, 1), shifted(two, -1)]

    n_occ = occ_energy.shape[0]
    occ_pairs = (occ_energy[: pairs // n_occ, None] + occ_energy[None, :]).reshape(pairs)
    occ_rows = lax.dynamic_slice_in_dim(occ_pairs, cd_index * rows, rows)
    vir_a = lax.dynamic_slice_in_dim(vir_energy, ab_index * a_local, a_local)
    vir_d = lax.dynamic_slice_in_dim(vir_energy, cd_index * d_local, d_local)
    denom_rows = vir_a[None, :, None] + vir_energy[None, None, :] - occ_rows[:, None, None]
    vir_block = (vir_d[:, None] + vir_a[None, :]).reshape(-1, 1)
    denom_block = vir_block - occ_pairs[None, :]

    rounded = amplitudes.astype(jnp.bfloat16).astype(jnp.float32)
    both = jnp.stack([amplitudes, driving])
    mirror = lax.all_to_all(both, AB, split_axis=3, concat_axis=2, tiled=True)
    mirror = mirror.transpose(0, 1, 3, 2)
    rounded_mirror = mirror[0].astype(jnp.bfloat16).astype(jnp.float32)
    even = 0.5 * jnp.stack([rounded + rounded_mirror, both[1] + mirror[1]])
    blocks = pair_layout(even, n_cd)
    current, drive = blocks[0], blocks[1]
    inward = spread(current.astype(jnp.bfloat16), n_ab)

    place = jnp.stack([lax.axis_index("y"), lax.axis_index("k")])
    tiles, kept, sent = tiles_and_ladder(place, left, inward, y_blocks)
    chip = kept + lax.ppermute(sent, "k", [(0, 1), (1, 0)]).astype(jnp.float32)
    parts = lax.all_to_all(chip.astype(jnp.bfloat16), CD[:2], 0, 0, tiled=True)
    ladder = jnp.sum(parts.astype(jnp.float32), axis=0)
    current = current - (drive + denom_block * current + ladder) / denom_block

    inward = spread(current.astype(jnp.bfloat16), n_ab)
    second = lax.dot_general(
        inward, tiles, (((0,), (0,)), ((), ())), preferred_element_type=jnp.float32
    ).astype(jnp.bfloat16)
    high = ladder.astype(jnp.bfloat16)
    low = (ladder - high.astype(jnp.float32)).astype(jnp.bfloat16)
    extra = jnp.stack([high, low]).reshape(2 * ladder.shape[0], n_cd, rows).transpose(1, 2, 0)
    message = jnp.concatenate([second.reshape(n_cd, rows, -1), extra], axis=2)
    parts = lax.all_to_all(message, CD, 0, 0, tiled=True)
    wide = virtuals * a_local
    ladder_second = jnp.sum(parts[:, :, :wide].astype(jnp.float32), axis=0)
    ladder_second = ladder_second.reshape(rows, a_local, virtuals)
    ladder_first = parts[:, :, wide:].astype(jnp.float32).reshape(n_cd, rows, 2, d_local, a_local)
    ladder_first = jnp.sum(ladder_first, axis=2).transpose(1, 3, 0, 2).reshape(rows, a_local, virtuals)

    current = amplitudes - (driving + denom_rows * amplitudes + ladder_first) / denom_rows
    residual = driving + denom_rows * current + ladder_second
    return (current - residual / denom_rows, residual)


def solution(mesh):
    fine = Mesh(mesh.devices.reshape(8, 2, 8, 2, 2), AB + CD)
    placed = (P(AB, CD, None), P(CD, AB, None), P(CD, AB, None), P(), P())
    return jax.shard_map(
        local,
        mesh=fine,
        in_specs=placed,
        out_specs=(P(CD, AB, None), P(CD, AB, None)),
        check_vma=False,
    )
```

```python
import jax
import jax.numpy as jnp
from jax import lax
from jax.experimental import pallas as pl
from jax.experimental.pallas import tpu as pltpu
from jax.sharding import Mesh, PartitionSpec as P


AB = ("y", "xl")
CD = ("z", "xh", "k")


def pair_layout(messages, count, rows):
    n_cd = messages.shape[0]
    swapped = lax.all_to_all(messages, CD, 0, 0, tiled=True)
    swapped = swapped.reshape(n_cd, count, -1, rows).transpose(1, 2, 0, 3)
    return swapped.reshape(count, -1, n_cd * rows)


def spread(block, n_ab):
    copies = jnp.broadcast_to(block[None], (n_ab,) + block.shape)
    return lax.all_to_all(copies, AB, 0, 0, tiled=True).reshape(-1, block.shape[1])


LANES = 128
SHIFTS = ((0,), (4,), (2,), (-2,), (1, 5), (-1, 3))


def tile_kernel(at_ref, left_ref, inward_ref, *refs):
    n_blocks = len(SHIFTS)
    block_refs, (tiles_ref, kept_ref, sent_ref, piece_ref, gram_ref, tile_ref, sum_ref) = refs[:n_blocks], refs[n_blocks:]
    n_z, n_k, n_xh, block, aux_width = left_ref.shape
    a_local = 8
    rows = n_z * n_k * n_xh * block
    _, n_xl, d_local, b_local, _ = block_refs[0].shape
    n_y = piece_ref.shape[1]

    @pl.when(pl.program_id(0) == 0)
    def _():
        for shifts, block_ref in zip(SHIFTS, block_refs):
            for slot, shift in enumerate(shifts):
                y = (at_ref[0] + n_y - shift) % n_y
                for d in range(d_local):
                    for xl in range(n_xl):
                        rows_at = slice(xl * b_local, (xl + 1) * b_local)
                        piece_ref[d, y, rows_at, :] = block_ref[slot, xl, d]

    left = jnp.concatenate(
        [left_ref[z, k, xh] for z in range(n_z) for xh in range(n_xh) for k in range(n_k)], axis=0
    )
    gram = lax.dot_general(
        left, piece_ref[...].reshape(d_local * LANES, aux_width), (((1,), (1,)), ((), ())), preferred_element_type=jnp.float32
    )
    for d in range(d_local):
        gram_ref[d] = gram[:, d * LANES : (d + 1) * LANES]
    groups = rows // (a_local * 8)
    for a in range(a_local):
        for d in range(d_local):
            part = gram_ref[d, pl.ds(a, rows // a_local, stride=a_local), :]
            tile_ref[:, d, :, a * LANES : (a + 1) * LANES] = part.reshape(groups, 8, LANES)
    tiles = tile_ref[...].reshape(groups * d_local * 8, a_local * LANES).astype(jnp.bfloat16)
    tiles_ref[...] = tiles
    first = pl.program_id(0) == 0
    product = lax.dot_general(
        tiles, inward_ref[...], (((0,), (0,)), ((), ())), preferred_element_type=jnp.float32
    )
    for half in range(2):
        lanes = slice(half * LANES, (half + 1) * LANES)
        for a in range(a_local):
            out = product[a * LANES : (a + 1) * LANES, lanes]
            at = pl.ds(a, LANES, stride=a_local)
            before = sum_ref[half, at, :]
            sum_ref[half, at, :] = jnp.where(first, out, before + out)
        n_groups, size, _ = kept_ref.shape
        for group in range(n_groups):
            own = pl.multiple_of((2 * group + at_ref[1]) * size, size)
            other = pl.multiple_of((2 * group + 1 - at_ref[1]) * size, size)
            kept_ref[group, :, lanes] = sum_ref[half, pl.ds(own, size), :]
            sent_ref[group, :, lanes] = sum_ref[half, pl.ds(other, size), :].astype(jnp.bfloat16)


def tiles_and_ladder(place, left, inward, blocks):
    n_z, n_k, n_xh, block, aux_width = left.shape
    steps = 2
    contracted = inward.shape[0]
    wide = 8 * LANES
    part = contracted // steps
    halves = (n_z * n_xh, wide // (n_z * n_xh * n_k), inward.shape[1])
    _, n_xl, d_local, b_local, _ = blocks[0].shape
    n_y = sum(block.shape[0] for block in blocks)
    return pl.pallas_call(
        tile_kernel,
        grid=(steps,),
        in_specs=[
            pl.BlockSpec(memory_space=pltpu.SMEM),
            pl.BlockSpec((n_z // steps, n_k, n_xh, block, aux_width), lambda s: (s, 0, 0, 0, 0)),
            pl.BlockSpec((part, inward.shape[1]), lambda s: (s, 0)),
        ]
        + [pl.BlockSpec(block.shape, lambda s: (0,) * 5, pipeline_mode=pl.Buffered(1)) for block in blocks],
        out_specs=[
            pl.BlockSpec((part, wide), lambda s: (s, 0)),
            pl.BlockSpec(halves, lambda s: (0, 0, 0)),
            pl.BlockSpec(halves, lambda s: (0, 0, 0)),
        ],
        out_shape=[
            jax.ShapeDtypeStruct((contracted, wide), jnp.bfloat16),
            jax.ShapeDtypeStruct(halves, jnp.float32),
            jax.ShapeDtypeStruct(halves, jnp.bfloat16),
        ],
        scratch_shapes=[
            pltpu.VMEM((d_local, n_y, n_xl * b_local, aux_width), jnp.bfloat16),
            pltpu.VMEM((d_local, 2 * part, LANES), jnp.float32),
            pltpu.VMEM((part // (8 * d_local), d_local, 8, wide), jnp.float32),
            pltpu.VMEM((2, wide, LANES), jnp.float32),
        ],
        name="tiles_and_ladder",
    )(place, left, inward, *blocks)


def local(factors, amplitudes, driving, occ_energy, vir_energy):
    rows, a_local, virtuals = amplitudes.shape
    d_local, aux_width = factors.shape[1:]
    n_z, n_xh, n_k = (lax.axis_size(name) for name in CD)
    n_ab, n_cd = virtuals // a_local, virtuals // d_local
    pairs = rows * n_cd
    cd_index = lax.axis_index(CD)
    ab_index = lax.axis_index(AB)

    turned = factors.transpose(1, 0, 2)
    theirs = lax.ppermute(turned, "xl", [(0, 1), (1, 0)])
    across = lax.ppermute(turned, "xh", [(0, 1), (1, 0)])
    low_member = lax.axis_index("xh") == 0
    columns = jnp.stack([jnp.where(low_member, turned, across), jnp.where(low_member, across, turned)])
    left = lax.all_gather(columns[None], ("z", "k"), axis=0, tiled=True)
    left = left.reshape(n_z, n_k, n_xh, d_local * a_local, aux_width)
    even_member = lax.axis_index("xl") == 0
    pair = jnp.stack([jnp.where(even_member, turned, theirs), jnp.where(even_member, theirs, turned)])
    n_y = lax.axis_size("y")

    def shifted(value, shift):
        return lax.ppermute(value, "y", [(i, (i + shift) % n_y) for i in range(n_y)])

    pair = pair[None]
    opposite = shifted(pair, 4)
    two = jnp.concatenate([pair, opposite])
    y_blocks = [pair, opposite, shifted(pair, 2), shifted(pair, -2), shifted(two, 1), shifted(two, -1)]

    n_occ = occ_energy.shape[0]
    occ_pairs = (occ_energy[: pairs // n_occ, None] + occ_energy[None, :]).reshape(pairs)
    occ_rows = lax.dynamic_slice_in_dim(occ_pairs, cd_index * rows, rows)
    vir_a = lax.dynamic_slice_in_dim(vir_energy, ab_index * a_local, a_local)
    vir_d = lax.dynamic_slice_in_dim(vir_energy, cd_index * d_local, d_local)
    denom_rows = vir_a[None, :, None] + vir_energy[None, None, :] - occ_rows[:, None, None]
    vir_block = (vir_d[:, None] + vir_a[None, :]).reshape(-1, 1)
    denom_block = vir_block - occ_pairs[None, :]

    rounded = amplitudes.astype(jnp.bfloat16).astype(jnp.float32)
    both = jnp.stack([rounded, driving])
    own = both.reshape(2, rows, a_local, n_cd, d_local).transpose(3, 0, 4, 2, 1).reshape(n_cd, -1, 128)
    outgoing = both.reshape(2, rows, n_cd // n_ab, d_local, n_ab, a_local).transpose(4, 2, 0, 3, 5, 1)
    mirror = lax.all_to_all(outgoing.reshape(n_ab, -1, 128), AB, 0, 0, tiled=True)
    even = 0.5 * (own + mirror.reshape(own.shape))
    blocks = pair_layout(even, 2, rows)
    current, drive = blocks[0], blocks[1]
    inward = spread(current.astype(jnp.bfloat16), n_ab)

    place = jnp.stack([lax.axis_index("y"), lax.axis_index("k")])
    tiles, kept, sent = tiles_and_ladder(place, left, inward, y_blocks)
    chip = kept + lax.ppermute(sent, "k", [(0, 1), (1, 0)]).astype(jnp.float32)
    parts = lax.all_to_all(chip.astype(jnp.bfloat16), CD[:2], 0, 0, tiled=True)
    ladder = jnp.sum(parts.astype(jnp.float32), axis=0)
    current = current - (drive + denom_block * current + ladder) / denom_block

    inward = spread(current.astype(jnp.bfloat16), n_ab)
    second = lax.dot_general(
        inward, tiles, (((0,), (0,)), ((), ())), preferred_element_type=jnp.float32
    ).astype(jnp.bfloat16)
    high = ladder.astype(jnp.bfloat16)
    low = (ladder - high.astype(jnp.float32)).astype(jnp.bfloat16)
    extra = jnp.stack([high, low]).reshape(2 * ladder.shape[0], n_cd, rows).transpose(1, 2, 0)
    message = jnp.concatenate([second.reshape(n_cd, rows, -1), extra], axis=2)
    parts = lax.all_to_all(message, CD, 0, 0, tiled=True)
    wide = virtuals * a_local
    ladder_second = jnp.sum(parts[:, :, :wide].astype(jnp.float32), axis=0)
    ladder_second = ladder_second.reshape(rows, a_local, virtuals)
    ladder_first = parts[:, :, wide:].astype(jnp.float32).reshape(n_cd, rows, 2, d_local, a_local)
    ladder_first = jnp.sum(ladder_first, axis=2).transpose(1, 3, 0, 2).reshape(rows, a_local, virtuals)

    current = amplitudes - (driving + denom_rows * amplitudes + ladder_first) / denom_rows
    residual = driving + denom_rows * current + ladder_second
    return (current - residual / denom_rows, residual)


def solution(mesh):
    fine = Mesh(mesh.devices.reshape(8, 2, 8, 2, 2), AB + CD)
    placed = (P(AB, CD, None), P(CD, AB, None), P(CD, AB, None), P(), P())
    return jax.shard_map(
        local,
        mesh=fine,
        in_specs=placed,
        out_specs=(P(CD, AB, None), P(CD, AB, None)),
        check_vma=False,
    )
```

```python
import jax
import jax.numpy as jnp
from jax import lax
from jax.experimental import pallas as pl
from jax.experimental.pallas import tpu as pltpu
from jax.sharding import Mesh, PartitionSpec as P


AB = ("y", "xl")
CD = ("z", "xh", "k")


def pair_layout(messages, count, rows):
    n_cd = messages.shape[0]
    swapped = lax.all_to_all(messages, CD, 0, 0, tiled=True)
    swapped = swapped.reshape(n_cd, count, -1, rows).transpose(1, 2, 0, 3)
    return swapped.reshape(count, -1, n_cd * rows)


def spread(block, n_ab):
    copies = jnp.broadcast_to(block[None], (n_ab,) + block.shape)
    return lax.all_to_all(copies, AB, 0, 0, tiled=True).reshape(-1, block.shape[1])


LANES = 128
SHIFTS = ((0,), (4,), (2,), (-2,), (1, 5), (-1, 3))


def tile_kernel(y_ref, left_ref, *refs):
    n_blocks = len(SHIFTS)
    block_refs = refs[:n_blocks]
    tiles_ref, turned_ref, piece_ref, gram_ref, tile_ref, wide_ref = refs[n_blocks:]
    n_z, n_k, n_xh, block, aux_width = left_ref.shape
    a_local = 8
    rows = n_z * n_k * n_xh * block
    _, n_xl, d_local, b_local, _ = block_refs[0].shape
    n_y = piece_ref.shape[1]

    @pl.when(pl.program_id(0) == 0)
    def _():
        for shifts, block_ref in zip(SHIFTS, block_refs):
            for slot, shift in enumerate(shifts):
                y = (y_ref[0] + n_y - shift) % n_y
                for d in range(d_local):
                    for xl in range(n_xl):
                        rows_at = slice(xl * b_local, (xl + 1) * b_local)
                        piece_ref[d, y, rows_at, :] = block_ref[slot, xl, d]

    left = jnp.concatenate(
        [left_ref[z, k, xh] for z in range(n_z) for xh in range(n_xh) for k in range(n_k)], axis=0
    )
    gram = lax.dot_general(
        left,
        piece_ref[...].reshape(d_local * LANES, aux_width),
        (((1,), (1,)), ((), ())),
        preferred_element_type=jnp.float32,
    )
    for d in range(d_local):
        gram_ref[d] = gram[:, d * LANES : (d + 1) * LANES]
    groups = rows // (a_local * 8)
    part = groups * d_local * 8
    for a in range(a_local):
        lanes = slice(a * LANES, (a + 1) * LANES)
        for d in range(d_local):
            piece = gram_ref[d, pl.ds(a, rows // a_local, stride=a_local), :]
            tile_ref[:, d, :, lanes] = piece.reshape(groups, 8, LANES)
        turned = tile_ref[:, :, :, lanes].reshape(part, LANES).T
        for half in range(part // LANES):
            at = pl.ds(a, LANES, stride=a_local)
            wide_ref[half, at, :] = turned[:, half * LANES : (half + 1) * LANES]
    tiles_ref[...] = tile_ref[...].reshape(part, a_local * LANES).astype(jnp.bfloat16)
    for half in range(part // LANES):
        turned_ref[:, half * LANES : (half + 1) * LANES] = wide_ref[half].astype(jnp.bfloat16)


def integral_tiles(y_index, left, blocks):
    n_z, n_k, n_xh, block, aux_width = left.shape
    steps = 2
    _, n_xl, d_local, b_local, _ = blocks[0].shape
    n_y = sum(value.shape[0] for value in blocks)
    wide = 8 * LANES
    contracted = n_z * n_k * n_xh * block * d_local // 8
    part = contracted // steps
    return pl.pallas_call(
        tile_kernel,
        grid=(steps,),
        in_specs=[
            pl.BlockSpec(memory_space=pltpu.SMEM),
            pl.BlockSpec((n_z // steps, n_k, n_xh, block, aux_width), lambda s: (s, 0, 0, 0, 0)),
        ]
        + [pl.BlockSpec(value.shape, lambda s: (0,) * 5, pipeline_mode=pl.Buffered(1)) for value in blocks],
        out_specs=[
            pl.BlockSpec((part, wide), lambda s: (s, 0)),
            pl.BlockSpec((wide, part), lambda s: (0, s)),
        ],
        out_shape=[
            jax.ShapeDtypeStruct((contracted, wide), jnp.bfloat16),
            jax.ShapeDtypeStruct((wide, contracted), jnp.bfloat16),
        ],
        scratch_shapes=[
            pltpu.VMEM((d_local, n_y, n_xl * b_local, aux_width), jnp.bfloat16),
            pltpu.VMEM((d_local, 2 * part, LANES), jnp.float32),
            pltpu.VMEM((part // (8 * d_local), d_local, 8, wide), jnp.float32),
            pltpu.VMEM((part // LANES, wide, LANES), jnp.float32),
        ],
        name="integral_tiles",
    )(y_index.reshape(1), left, *blocks)


def ladder_kernel(k_ref, turned_ref, inward_ref, kept_ref, sent_ref, sum_ref):
    sum_ref[...] = jnp.dot(turned_ref[...], inward_ref[...], preferred_element_type=jnp.float32)
    n_groups, size, _ = kept_ref.shape
    for group in range(n_groups):
        own = pl.multiple_of((2 * group + k_ref[0]) * size, size)
        other = pl.multiple_of((2 * group + 1 - k_ref[0]) * size, size)
        kept_ref[group] = sum_ref[pl.ds(own, size), :]
        sent_ref[group] = sum_ref[pl.ds(other, size), :].astype(jnp.bfloat16)


def first_ladder(k_index, turned, inward, groups):
    wide, pairs = turned.shape[0], inward.shape[1]
    halves = (groups, wide // (2 * groups), pairs)
    whole = pl.BlockSpec(memory_space=pltpu.VMEM)
    return pl.pallas_call(
        ladder_kernel,
        in_specs=[pl.BlockSpec(memory_space=pltpu.SMEM), whole, whole],
        out_specs=[whole, whole],
        out_shape=[
            pltpu.VMEM(halves, jnp.float32),
            pltpu.VMEM(halves, jnp.bfloat16),
        ],
        scratch_shapes=[pltpu.VMEM((wide, pairs), jnp.float32)],
        name="first_ladder",
    )(
        k_index.reshape(1),
        pltpu.with_memory_space_constraint(turned, pltpu.VMEM),
        pltpu.with_memory_space_constraint(inward, pltpu.VMEM),
    )


def local(factors, amplitudes, driving, occ_energy, vir_energy):
    rows, a_local, virtuals = amplitudes.shape
    d_local, aux_width = factors.shape[1:]
    n_z, n_xh, n_k = (lax.axis_size(name) for name in CD)
    n_ab, n_cd = virtuals // a_local, virtuals // d_local
    pairs = rows * n_cd
    cd_index = lax.axis_index(CD)
    ab_index = lax.axis_index(AB)

    turned = factors.transpose(1, 0, 2)
    theirs = lax.ppermute(turned, "xl", [(0, 1), (1, 0)])
    across = lax.ppermute(turned, "xh", [(0, 1), (1, 0)])
    low_member = lax.axis_index("xh") == 0
    columns = jnp.stack([jnp.where(low_member, turned, across), jnp.where(low_member, across, turned)])
    left = lax.all_gather(columns[None], ("z", "k"), axis=0, tiled=True)
    left = left.reshape(n_z, n_k, n_xh, d_local * a_local, aux_width)
    even_member = lax.axis_index("xl") == 0
    pair = jnp.stack([jnp.where(even_member, turned, theirs), jnp.where(even_member, theirs, turned)])
    n_y = lax.axis_size("y")

    def shifted(value, shift):
        return lax.ppermute(value, "y", [(i, (i + shift) % n_y) for i in range(n_y)])

    pair = pair[None]
    opposite = shifted(pair, 4)
    two = jnp.concatenate([pair, opposite])
    y_blocks = [pair, opposite, shifted(pair, 2), shifted(pair, -2), shifted(two, 1), shifted(two, -1)]

    n_occ = occ_energy.shape[0]
    occ_pairs = (occ_energy[: pairs // n_occ, None] + occ_energy[None, :]).reshape(pairs)
    occ_rows = lax.dynamic_slice_in_dim(occ_pairs, cd_index * rows, rows)
    vir_a = lax.dynamic_slice_in_dim(vir_energy, ab_index * a_local, a_local)
    vir_d = lax.dynamic_slice_in_dim(vir_energy, cd_index * d_local, d_local)
    denom_rows = vir_a[None, :, None] + vir_energy[None, None, :] - occ_rows[:, None, None]
    vir_block = (vir_d[:, None] + vir_a[None, :]).reshape(-1, 1)
    denom_block = vir_block - occ_pairs[None, :]

    rounded = amplitudes.astype(jnp.bfloat16).astype(jnp.float32)
    both = jnp.stack([rounded, driving])
    own = both.reshape(2, rows, a_local, n_cd, d_local).transpose(3, 0, 4, 2, 1).reshape(n_cd, -1, 128)
    outgoing = both.reshape(2, rows, n_cd // n_ab, d_local, n_ab, a_local).transpose(4, 2, 0, 3, 5, 1)
    mirror = lax.all_to_all(outgoing.reshape(n_ab, -1, 128), AB, 0, 0, tiled=True)
    even = 0.5 * (own + mirror.reshape(own.shape))
    blocks = pair_layout(even, 2, rows)
    current, drive = blocks[0], blocks[1]
    inward = spread(current.astype(jnp.bfloat16), n_ab)

    tiles, turned_tiles = integral_tiles(lax.axis_index("y"), left, y_blocks)
    kept, sent = first_ladder(lax.axis_index("k"), turned_tiles, inward, n_z * n_xh)
    chip = kept + lax.ppermute(sent, "k", [(0, 1), (1, 0)]).astype(jnp.float32)
    parts = lax.all_to_all(chip.astype(jnp.bfloat16), CD[:2], 0, 0, tiled=True)
    ladder = jnp.sum(parts.astype(jnp.float32), axis=0)
    current = current - (drive + denom_block * current + ladder) / denom_block

    inward = spread(current.astype(jnp.bfloat16), n_ab)
    second = lax.dot_general(
        inward, tiles, (((0,), (0,)), ((), ())), preferred_element_type=jnp.float32
    ).astype(jnp.bfloat16)
    high = ladder.astype(jnp.bfloat16)
    low = (ladder - high.astype(jnp.float32)).astype(jnp.bfloat16)
    extra = jnp.stack([high, low]).reshape(2 * ladder.shape[0], n_cd, rows).transpose(1, 2, 0)
    message = jnp.concatenate([second.reshape(n_cd, rows, -1), extra], axis=2)
    parts = lax.all_to_all(message, CD, 0, 0, tiled=True)
    wide = virtuals * a_local
    ladder_second = jnp.sum(parts[:, :, :wide].astype(jnp.float32), axis=0)
    ladder_second = ladder_second.reshape(rows, a_local, virtuals)
    ladder_first = parts[:, :, wide:].astype(jnp.float32).reshape(n_cd, rows, 2, d_local, a_local)
    ladder_first = jnp.sum(ladder_first, axis=2).transpose(1, 3, 0, 2).reshape(rows, a_local, virtuals)

    current = amplitudes - (driving + denom_rows * amplitudes + ladder_first) / denom_rows
    residual = driving + denom_rows * current + ladder_second
    return (current - residual / denom_rows, residual)


def solution(mesh):
    fine = Mesh(mesh.devices.reshape(8, 2, 8, 2, 2), AB + CD)
    placed = (P(AB, CD, None), P(CD, AB, None), P(CD, AB, None), P(), P())
    return jax.shard_map(
        local,
        mesh=fine,
        in_specs=placed,
        out_specs=(P(CD, AB, None), P(CD, AB, None)),
        check_vma=False,
    )
```

```python
import jax
import jax.numpy as jnp
from jax import lax
from jax.experimental import pallas as pl
from jax.experimental.pallas import tpu as pltpu
from jax.sharding import Mesh, PartitionSpec as P


AB = ("y", "xl")
CD = ("z", "xh", "k")


def pair_layout(messages, count, rows):
    n_cd = messages.shape[0]
    swapped = lax.all_to_all(messages, CD, 0, 0, tiled=True)
    swapped = swapped.reshape(n_cd, count, -1, rows).transpose(1, 2, 0, 3)
    return swapped.reshape(count, -1, n_cd * rows)


def spread(block, n_ab):
    copies = jnp.broadcast_to(block[None], (n_ab,) + block.shape)
    return lax.all_to_all(copies, AB, 0, 0, tiled=True).reshape(-1, block.shape[1])


LANES = 128
SHIFTS = ((0,), (4,), (2,), (-2,), (1, 5), (-1, 3))


WHOLE = pl.BlockSpec(memory_space=pltpu.VMEM)


def near(value):
    return pltpu.with_memory_space_constraint(value, pltpu.VMEM)


def tile_kernel(y_ref, left_ref, *refs):
    n_blocks = len(SHIFTS)
    block_refs = refs[:n_blocks]
    tiles_ref, turned_ref, piece_ref, gram_ref, tile_ref, wide_ref = refs[n_blocks:]
    n_z, n_k, n_xh, block, aux_width = left_ref.shape
    a_local = 8
    rows = n_z * n_k * n_xh * block
    _, n_xl, d_local, b_local, _ = block_refs[0].shape
    n_y = piece_ref.shape[1]

    @pl.when(pl.program_id(0) == 0)
    def _():
        for shifts, block_ref in zip(SHIFTS, block_refs):
            for slot, shift in enumerate(shifts):
                y = (y_ref[0] + n_y - shift) % n_y
                for d in range(d_local):
                    for xl in range(n_xl):
                        rows_at = slice(xl * b_local, (xl + 1) * b_local)
                        piece_ref[d, y, rows_at, :] = block_ref[slot, xl, d]

    left = jnp.concatenate(
        [left_ref[z, k, xh] for z in range(n_z) for xh in range(n_xh) for k in range(n_k)], axis=0
    )
    gram = lax.dot_general(
        left,
        piece_ref[...].reshape(d_local * LANES, aux_width),
        (((1,), (1,)), ((), ())),
        preferred_element_type=jnp.float32,
    )
    for d in range(d_local):
        gram_ref[d] = gram[:, d * LANES : (d + 1) * LANES]
    groups = rows // (a_local * 8)
    part = groups * d_local * 8
    for a in range(a_local):
        lanes = slice(a * LANES, (a + 1) * LANES)
        for d in range(d_local):
            piece = gram_ref[d, pl.ds(a, rows // a_local, stride=a_local), :]
            tile_ref[:, d, :, lanes] = piece.reshape(groups, 8, LANES)
        turned = tile_ref[:, :, :, lanes].reshape(part, LANES).T
        for half in range(part // LANES):
            at = pl.ds(a, LANES, stride=a_local)
            wide_ref[half, at, :] = turned[:, half * LANES : (half + 1) * LANES]
    start = pl.multiple_of(pl.program_id(0) * part, part)
    tiles_ref[pl.ds(start, part), :] = tile_ref[...].reshape(part, a_local * LANES).astype(jnp.bfloat16)
    for half in range(part // LANES):
        turned_ref[:, pl.ds(start + half * LANES, LANES)] = wide_ref[half].astype(jnp.bfloat16)


def integral_tiles(y_index, left, blocks):
    n_z, n_k, n_xh, block, aux_width = left.shape
    steps = 2
    _, n_xl, d_local, b_local, _ = blocks[0].shape
    n_y = sum(value.shape[0] for value in blocks)
    wide = 8 * LANES
    contracted = n_z * n_k * n_xh * block * d_local // 8
    part = contracted // steps
    return pl.pallas_call(
        tile_kernel,
        grid=(steps,),
        in_specs=[
            pl.BlockSpec(memory_space=pltpu.SMEM),
            pl.BlockSpec((n_z // steps, n_k, n_xh, block, aux_width), lambda s: (s, 0, 0, 0, 0)),
        ]
        + [pl.BlockSpec(value.shape, lambda s: (0,) * 5, pipeline_mode=pl.Buffered(1)) for value in blocks],
        out_specs=[WHOLE, WHOLE],
        out_shape=[
            pltpu.VMEM((contracted, wide), jnp.bfloat16),
            pltpu.VMEM((wide, contracted), jnp.bfloat16),
        ],
        scratch_shapes=[
            pltpu.VMEM((d_local, n_y, n_xl * b_local, aux_width), jnp.bfloat16),
            pltpu.VMEM((d_local, 2 * part, LANES), jnp.float32),
            pltpu.VMEM((part // (8 * d_local), d_local, 8, wide), jnp.float32),
            pltpu.VMEM((part // LANES, wide, LANES), jnp.float32),
        ],
        name="integral_tiles",
    )(y_index.reshape(1), left, *blocks)


def ladder_kernel(k_ref, turned_ref, inward_ref, kept_ref, sent_ref, sum_ref):
    sum_ref[...] = jnp.dot(turned_ref[...], inward_ref[...], preferred_element_type=jnp.float32)
    n_groups, size, _ = kept_ref.shape
    for group in range(n_groups):
        own = pl.multiple_of((2 * group + k_ref[0]) * size, size)
        other = pl.multiple_of((2 * group + 1 - k_ref[0]) * size, size)
        kept_ref[group] = sum_ref[pl.ds(own, size), :]
        sent_ref[group] = sum_ref[pl.ds(other, size), :].astype(jnp.bfloat16)


def first_ladder(k_index, turned, inward, groups):
    wide, pairs = turned.shape[0], inward.shape[1]
    halves = (groups, wide // (2 * groups), pairs)
    return pl.pallas_call(
        ladder_kernel,
        in_specs=[pl.BlockSpec(memory_space=pltpu.SMEM), WHOLE, WHOLE],
        out_specs=[WHOLE, WHOLE],
        out_shape=[
            pltpu.VMEM(halves, jnp.float32),
            pltpu.VMEM(halves, jnp.bfloat16),
        ],
        scratch_shapes=[pltpu.VMEM((wide, pairs), jnp.float32)],
        compiler_params=pltpu.CompilerParams(vmem_limit_bytes=16 << 20),
        name="first_ladder",
    )(
        k_index.reshape(1),
        near(turned),
        near(inward),
    )


def second_kernel(tiles_ref, inward_ref, extra_ref, message_ref):
    product = lax.dot_general(
        inward_ref[...], tiles_ref[...], (((0,), (0,)), ((), ())), preferred_element_type=jnp.float32
    )
    members, rows, _ = extra_ref.shape
    wide = tiles_ref.shape[1]
    message_ref[:, :, :wide] = product.astype(jnp.bfloat16).reshape(members, rows, wide)
    message_ref[:, :, wide:] = extra_ref[...]


def second_ladder(tiles, inward, extra):
    members, rows, width = extra.shape
    return pl.pallas_call(
        second_kernel,
        in_specs=[WHOLE, WHOLE, WHOLE],
        out_specs=WHOLE,
        out_shape=pltpu.VMEM((members, rows, tiles.shape[1] + width), jnp.bfloat16),
        compiler_params=pltpu.CompilerParams(vmem_limit_bytes=16 << 20),
        name="second_ladder",
    )(near(tiles), near(inward), near(extra))


def local(factors, amplitudes, driving, occ_energy, vir_energy):
    rows, a_local, virtuals = amplitudes.shape
    d_local, aux_width = factors.shape[1:]
    n_z, n_xh, n_k = (lax.axis_size(name) for name in CD)
    n_ab, n_cd = virtuals // a_local, virtuals // d_local
    pairs = rows * n_cd
    cd_index = lax.axis_index(CD)
    ab_index = lax.axis_index(AB)

    turned = factors.transpose(1, 0, 2)
    theirs = lax.ppermute(turned, "xl", [(0, 1), (1, 0)])
    across = lax.ppermute(turned, "xh", [(0, 1), (1, 0)])
    low_member = lax.axis_index("xh") == 0
    columns = jnp.stack([jnp.where(low_member, turned, across), jnp.where(low_member, across, turned)])
    left = lax.all_gather(columns[None], ("z", "k"), axis=0, tiled=True)
    left = left.reshape(n_z, n_k, n_xh, d_local * a_local, aux_width)
    even_member = lax.axis_index("xl") == 0
    pair = jnp.stack([jnp.where(even_member, turned, theirs), jnp.where(even_member, theirs, turned)])
    n_y = lax.axis_size("y")

    def shifted(value, shift):
        return lax.ppermute(value, "y", [(i, (i + shift) % n_y) for i in range(n_y)])

    pair = pair[None]
    opposite = shifted(pair, 4)
    two = jnp.concatenate([pair, opposite])
    y_blocks = [pair, opposite, shifted(pair, 2), shifted(pair, -2), shifted(two, 1), shifted(two, -1)]

    n_occ = occ_energy.shape[0]
    occ_pairs = (occ_energy[: pairs // n_occ, None] + occ_energy[None, :]).reshape(pairs)
    occ_rows = lax.dynamic_slice_in_dim(occ_pairs, cd_index * rows, rows)
    vir_a = lax.dynamic_slice_in_dim(vir_energy, ab_index * a_local, a_local)
    vir_d = lax.dynamic_slice_in_dim(vir_energy, cd_index * d_local, d_local)
    denom_rows = vir_a[None, :, None] + vir_energy[None, None, :] - occ_rows[:, None, None]
    vir_block = (vir_d[:, None] + vir_a[None, :]).reshape(-1, 1)
    denom_block = vir_block - occ_pairs[None, :]

    rounded = amplitudes.astype(jnp.bfloat16).astype(jnp.float32)
    both = jnp.stack([rounded, driving])
    own = both.reshape(2, rows, a_local, n_cd, d_local).transpose(3, 0, 4, 2, 1).reshape(n_cd, -1, 128)
    outgoing = both.reshape(2, rows, n_cd // n_ab, d_local, n_ab, a_local).transpose(4, 2, 0, 3, 5, 1)
    outgoing = outgoing.reshape(n_ab, -1, 128)
    mirror = lax.all_to_all(outgoing, AB, 0, 0, tiled=True)
    even = 0.5 * (own + mirror.reshape(own.shape))
    blocks = pair_layout(even, 2, rows)
    current, drive = blocks[0], blocks[1]
    inward = spread(current.astype(jnp.bfloat16), n_ab)

    tiles, turned_tiles = integral_tiles(lax.axis_index("y"), left, y_blocks)
    kept, sent = first_ladder(lax.axis_index("k"), turned_tiles, inward, n_z * n_xh)
    chip = kept + lax.ppermute(sent, "k", [(0, 1), (1, 0)]).astype(jnp.float32)
    parts = lax.all_to_all(chip.astype(jnp.bfloat16), CD[:2], 0, 0, tiled=True)
    ladder = jnp.sum(parts.astype(jnp.float32), axis=0)
    current = current - (drive + denom_block * current + ladder) / denom_block

    inward = spread(current.astype(jnp.bfloat16), n_ab)
    high = ladder.astype(jnp.bfloat16)
    low = (ladder - high.astype(jnp.float32)).astype(jnp.bfloat16)
    extra = jnp.stack([high, low]).reshape(2 * ladder.shape[0], n_cd, rows).transpose(1, 2, 0)
    message = second_ladder(tiles, inward, extra)
    parts = lax.all_to_all(message, CD, 0, 0, tiled=True)
    wide = virtuals * a_local
    ladder_second = jnp.sum(parts[:, :, :wide].astype(jnp.float32), axis=0)
    ladder_second = ladder_second.reshape(rows, a_local, virtuals)
    ladder_first = parts[:, :, wide:].astype(jnp.float32).reshape(n_cd, rows, 2, d_local, a_local)
    ladder_first = jnp.sum(ladder_first, axis=2).transpose(1, 3, 0, 2).reshape(rows, a_local, virtuals)

    current = amplitudes - (driving + denom_rows * amplitudes + ladder_first) / denom_rows
    residual = driving + denom_rows * current + ladder_second
    return (current - residual / denom_rows, residual)


def solution(mesh):
    fine = Mesh(mesh.devices.reshape(8, 2, 8, 2, 2), AB + CD)
    placed = (P(AB, CD, None), P(CD, AB, None), P(CD, AB, None), P(), P())
    return jax.shard_map(
        local,
        mesh=fine,
        in_specs=placed,
        out_specs=(P(CD, AB, None), P(CD, AB, None)),
        check_vma=False,
    )
```
